256 devices in a mesh: dp: 8 (over y, x_hi), mp: 32 (over z, x_lo, core).
Axes of the slice: x: 4 (x_hi: 2, x_lo: 2; x = x_hi * 2 + x_lo), y: 4, z: 8, core: 2. Of those that a mesh axis runs over, the one named last changes fastest.
Arguments:
- activations: bfloat16 [4096, 4096], P('dp', 'mp'), may hold values from -22 to 22
- out_grads: bfloat16 [4096, 32768], P('dp', 'mp'), may hold values from -1 to 1
- weight: float32 [4096, 32768], P('dp', 'mp'), may hold values from -0.09375 to 0.09375
- row_state: float32 [4096], P('dp'), may hold values from 0.1 to 1.6
- column_state: float32 [32768], P('mp'), may hold values from 0.1 to 1.6
- next_batch: bfloat16 [4096, 4096], P('dp', 'mp'), may hold values from -6 to 6
Outputs:
- new_weight: float32 [4096, 32768], P('dp', 'mp')
- update: float32 [4096, 32768], P('dp', 'mp')
- row_moment: float32 [4096], P('dp')
- column_moment: float32 [32768], P('mp')
- next_hidden: bfloat16 [4096, 32768], P('dp', 'mp')
The draws below stay inside these ranges and needn't reach their ends.
All inputs are finite; a program needn't handle non-finite values.
Results may differ from the reference program's by a relative error of at most 0.001.
The reference program's roundings to bfloat16 on the way (of `weight_half`) count: a program that leaves them out, or rounds other values in their place, can miss the bound.
Values may be sent and summed in bfloat16 or wider, within the bound.
A program may use at most 128 MiB of HBM per device.

```python
import math
import jax
import jax.numpy as jnp
from jax import lax

D = 4096
FF = 32768
TOKENS = 4096


def column_scales(key, number):
    place = jnp.arange(number, dtype=jnp.float32) / number
    spread = jax.random.uniform(key, (number,), jnp.float32, -0.5, 0.5)
    return 3.0 ** (place - 0.5) * 10.0 ** spread


def scaled_rows(key, width):
    keys = jax.random.split(key, 2)
    scales = column_scales(keys[0], width)
    values = jnp.clip(jax.random.normal(keys[1], (TOKENS, width), jnp.float32), -4.0, 4.0)
    return values * scales[None, :]


def draw_activations(key, part):
    values = scaled_rows(jax.random.fold_in(key, 11), D)
    return values.astype(jnp.bfloat16)


def draw_out_grads(key, part):
    values = scaled_rows(jax.random.fold_in(key, 23), FF)
    values = values / (3.0 * jnp.sqrt(jnp.float32(TOKENS)))
    return values.astype(jnp.bfloat16)


def block_levels(own_key, dims, cuts, low, high):
    level = 1.0
    for position, shards_of in cuts:
        steps = jax.random.uniform(jax.random.fold_in(jax.random.fold_in(own_key, 6), position), (shards_of,), jnp.float32, low / len(cuts), high / len(cuts))
        level = level * jnp.repeat(jnp.exp(steps), dims[position] // shards_of).reshape((-1,) + (1,) * (len(dims) - 1 - position))
    return level


def normal_values(stream_key, extent, deviation, limit, cuts=(), kind=jnp.bfloat16):
    result = deviation * jax.random.normal(stream_key, extent, jnp.float32)
    if cuts:
        result = result * block_levels(stream_key, extent, cuts, -0.22, 0.18)
    return jnp.clip(result, -limit, limit).astype(kind)


def setup_inputs(seed: int = 0) -> dict:
    arg_keys = jax.random.split(jax.random.key(seed), 7)
    activations = draw_activations(jax.random.fold_in(arg_keys[6], 71), 0)
    out_grads = draw_out_grads(jax.random.fold_in(arg_keys[6], 71), 0)
    weight = normal_values(arg_keys[2], (D, FF), D ** -0.5, 0.09375, ((0, 8), (1, 32)), jnp.float32)
    row_state = jnp.clip(jnp.exp(math.log(1.6) - 2.7725887 * jax.random.uniform(arg_keys[3], (D,), jnp.float32) ** block_levels(arg_keys[3], (D,), ((0, 8),), -0.2, 0.2)), 0.1, 1.6)
    column_state = jnp.clip(jnp.exp(math.log(1.6) - 2.7725887 * jax.random.uniform(arg_keys[4], (FF,), jnp.float32) ** block_levels(arg_keys[4], (FF,), ((0, 32),), -0.2, 0.2)), 0.1, 1.6)
    next_batch = normal_values(arg_keys[5], (TOKENS, D), 1.0, 6.0, ((0, 8), (1, 32)))
    return {"activations": activations, "out_grads": out_grads, "weight": weight, "row_state": row_state, "column_state": column_state, "next_batch": next_batch}


tiny_square = 1e-30
weight_eps = 1e-06
decay_rate = 0.5
clip_level = 0.5
learn_rate = 0.01

def reference(activations, out_grads, weight, row_state, column_state, next_batch):
    gradient = jnp.dot(activations.T, out_grads, preferred_element_type=jnp.float32)
    squares = gradient * gradient + tiny_square
    row_moment = decay_rate * row_state + (1.0 - decay_rate) * lax.optimization_barrier(jnp.mean(squares, axis=1))
    column_moment = decay_rate * column_state + (1.0 - decay_rate) * lax.optimization_barrier(jnp.mean(squares, axis=0))
    raw_update = gradient * lax.rsqrt(row_moment[:, None] * column_moment[None, :])
    rms_update = jnp.sqrt(jnp.mean(raw_update * raw_update))
    update = raw_update / jnp.maximum(1.0, rms_update / clip_level)
    rms_weight = jnp.sqrt(jnp.mean(weight * weight) + weight_eps)
    new_weight = weight - learn_rate * rms_weight * update
    weight_half = new_weight.astype(jnp.bfloat16)
    next_hidden = jnp.dot(next_batch, weight_half, preferred_element_type=jnp.float32).astype(jnp.bfloat16)
    return (new_weight, update, row_moment, column_moment, next_hidden)
```

```python
import functools
import heapq

import jax
import jax.numpy as jnp
from jax import lax
from jax.experimental import pallas as pl
from jax.experimental.pallas import tpu as pltpu
from jax.sharding import PartitionSpec as P

D = 4096
FF = 32768

tiny_square = 1e-30
weight_eps = 1e-06
decay_rate = 0.5
clip_level = 0.5
learn_rate = 0.01

ROWS = 512
COLS = 1024
W = 128
CHUNKS = COLS // W
Y_FIRST = (0, 1, 2)
X_FIRST = (3, 4, 5, 6, 7)
COPIES = 400
RELAYS = 2 * (len(X_FIRST) + 4 * len(Y_FIRST))

HOP_US = 1.7
RATE = 46e3
DOT_US = 1.6

F32 = jnp.float32
BF16 = jnp.bfloat16
MESH = pl.DeviceIdType.MESH


class Place:
    def __init__(self):
        self.dp = lax.axis_index("dp")
        self.mp = lax.axis_index("mp")
        self.y = self.dp // 2
        self.xh = self.dp % 2
        self.z = self.mp // 4
        self.xl = (self.mp // 2) % 2
        self.core = self.mp % 2
        self.x = 2 * self.xh + self.xl

    def device(self, dy=0, dx=0, dz=0, dcore=0):
        y = (self.y + dy) % 4
        x = (self.x + dx) % 4
        z = (self.z + dz) % 8
        core = (self.core + dcore) % 2
        return (2 * y + x // 2, 4 * z + 2 * (x % 2) + core)


class Net:
    def __init__(self, send_sems, recv_sems):
        self.send_sems, self.recv_sems = send_sems, recv_sems
        self.copies, self.heap, self.free = [], [], {}
        self.now = 0.0
        self.first = 0

    def send(self, link, src, dst, device, size, then, hop=HOP_US):
        k = len(self.copies)
        copy = pltpu.make_async_remote_copy(
            src_ref=src, dst_ref=dst, send_sem=self.send_sems.at[k], recv_sem=self.recv_sems.at[k],
            device_id=device, device_id_type=MESH)
        copy.start()
        self.copies.append(copy)
        begin = max(self.free.get(link, 0.0), self.now)
        end = begin + size / (RATE * (12 if link == "core" else 1))
        self.free[link] = end
        heapq.heappush(self.heap, (end + hop, k, copy, then))

    def run(self, until=None):
        while self.heap and not (until and until()):
            at, _, copy, then = heapq.heappop(self.heap)
            self.now = max(self.now, at)
            copy.wait_recv()
            if then is not None:
                then()

    def finish(self):
        for copy in self.copies[self.first:]:
            copy.wait_send()
        self.first = len(self.copies)


def block(ref, c, t, half=None):
    if half is None:
        return ref.at[c, pl.ds(pl.multiple_of(t * ROWS, ROWS), ROWS), :]
    rows = ROWS // 2
    return ref.at[c, pl.ds(pl.multiple_of(t * ROWS + half * rows, rows), rows), :]


class GatherDp:
    FULL = ROWS * W * 2

    def __init__(self, net, me, buf, relay, done):
        self.net, self.me, self.buf, self.relay, self.done = net, me, buf, relay, done
        self.left = {c: 10 for c in X_FIRST}
        self.left.update({c: 12 for c in Y_FIRST})
        self.relays = 0
        self.partner_halves = {c: 0 for c in X_FIRST}

    def index(self, dy, other):
        xh = (self.me.xh + 1) % 2 if other else self.me.xh
        return 2 * ((self.me.y + dy) % 4) + xh

    def got(self, c):
        self.left[c] -= 1
        if self.left[c] == 0:
            self.done(c)

    def along_y(self, c, other):
        for sign in (1, -1):
            part = block(self.buf, c, self.index(0, other))
            self.net.send(("y", sign), part, part, self.me.device(dy=sign), self.FULL,
                          functools.partial(self.from_y, c, other, sign))

    def from_y(self, c, other, sign):
        half = 0 if sign == 1 else 1
        part = block(self.buf, c, self.index(-sign, other), half)
        self.net.send(("y", sign), part, part, self.me.device(dy=sign), self.FULL // 2,
                      functools.partial(self.from_far_y, c, other, half))
        if c in Y_FIRST:
            self.along_x(c, -sign, 0)
            self.along_x(c, -sign, 1)
        self.got(c)

    def from_far_y(self, c, other, half):
        if c in Y_FIRST:
            self.along_x(c, 2, half)
        self.got(c)

    def along_x(self, c, dy, half):
        sign = 1 if half == 0 else -1
        slot = self.relay.at[self.relays]
        self.relays += 1
        self.net.send(("x", sign), block(self.buf, c, self.index(dy, False), half), slot,
                      self.me.device(dx=sign), self.FULL // 2,
                      functools.partial(self.relayed, c, dy, half, sign, slot))

    def relayed(self, c, dy, half, sign, slot):
        xh = ((self.me.x + 4 - sign) % 4) // 2
        t = 2 * ((self.me.y + dy) % 4) + xh
        self.net.send(("x", sign), slot, block(self.buf, c, t, half), self.me.device(dx=sign),
                      self.FULL // 2, functools.partial(self.from_x, c))

    def from_x(self, c):
        if c in X_FIRST:
            self.partner_halves[c] += 1
            if self.partner_halves[c] == 2:
                self.along_y(c, True)
        self.got(c)


class GatherMp:
    SIZE = ROWS * W * 2

    def __init__(self, net, me, strip, reach, done):
        self.net, self.me, self.strip, self.reach, self.done = net, me, strip, reach, done
        self.left = 31

    def got(self):
        self.left -= 1
        if self.left == 0:
            self.done()

    def place(self, dz, other):
        xl = (self.me.xl + 1) % 2 if other else self.me.xl
        return self.strip((self.me.z + dz) % 8, xl, self.me.core)

    def start(self):
        mine = self.place(0, False)
        dp, z, xl, core = self.me.dp, self.me.z, (self.me.xl + 1) % 2, self.me.core
        self.net.send(("x", 0), mine, mine, (dp, 4 * z + 2 * xl + core), self.SIZE, self.pair)
        self.have(0, False)

    def pair(self):
        self.have(0, True)
        self.got()

    def have(self, dz, other):
        part = self.place(dz, other)
        for sign in (1, -1):
            hops = -dz * sign
            if (dz == 0 or hops > 0) and hops < self.reach[sign]:
                self.net.send(("z", sign), part, part, self.me.device(dz=sign), self.SIZE,
                              functools.partial(self.from_z, dz - sign, other))
        self.net.send("core", part, part, self.me.device(dcore=1), self.SIZE, self.got, hop=1.0)

    def from_z(self, dz, other):
        self.have(dz, other)
        self.got()


def kernel(act, out_grads, weight, row_state, col_state, nxt,
           new_weight, update, row_out, col_out, hidden,
           act_v, nxt_v, act_t, pieces, at, xb, ob, wb, o_relay, w_relay,
           w_v, g_v, u_v, h_v, colbuf, rowbuf, tbuf, lastbuf,
           send_sems, recv_sems, a_send, a_recv, b_send, b_recv,
           col_send, col_recv, row_send, row_recv, t_send, t_recv, last_send, last_recv, local_sems):
    me = Place()
    dp, mp = me.dp, me.mp

    loads = [
        pltpu.make_async_copy(act, act_v, local_sems.at[0]),
        pltpu.make_async_copy(nxt, xb.at[:, pl.ds(pl.multiple_of(mp * W, W), W)], local_sems.at[1]),
        pltpu.make_async_copy(weight, w_v, local_sems.at[2]),
    ]
    for c in range(CHUNKS):
        loads.append(pltpu.make_async_copy(
            out_grads.at[:, pl.ds(c * W, W)], block(ob, c, dp), local_sems.at[3 + c]))
    for copy in loads:
        copy.start()

    barrier = pltpu.get_barrier_semaphore()

    def greet_mp(k, carry):
        pl.semaphore_signal(barrier, inc=1, device_id=(dp, (mp + k) % 32), device_id_type=MESH)
        return carry

    def greet_dp(k, carry):
        pl.semaphore_signal(barrier, inc=1, device_id=((dp + k) % 8, mp), device_id_type=MESH)
        return carry

    lax.fori_loop(1, 32, greet_mp, 0)
    lax.fori_loop(1, 8, greet_dp, 0)
    pl.semaphore_signal(barrier, inc=1, device_id=me.device(dx=2 * me.xl - 1), device_id_type=MESH)

    loads[0].wait()
    act_t[...] = act_v[...].T
    pieces[me.z] = act_t[pl.ds(pl.multiple_of(16 * me.z, 16), 16), :]
    pl.semaphore_wait(barrier, 39)

    def to_z(k):
        z = (me.z + k) % 8
        return pltpu.make_async_remote_copy(
            src_ref=act_t.at[pl.ds(pl.multiple_of(16 * z, 16), 16), :], dst_ref=pieces.at[me.z],
            send_sem=a_send.at[k], recv_sem=a_recv.at[k],
            device_id=(dp, (mp + 4 * k) % 32), device_id_type=MESH)

    strip_row = pl.multiple_of((2 * me.xl + me.core) * W + 16 * me.z, 16)

    def to_dp(k):
        i = (dp + k) % 8
        return pltpu.make_async_remote_copy(
            src_ref=pieces.at[i],
            dst_ref=at.at[pl.ds(strip_row, 16), pl.ds(pl.multiple_of(dp * ROWS, ROWS), ROWS)],
            send_sem=b_send.at[k], recv_sem=b_recv.at[k],
            device_id=(i, mp), device_id_type=MESH)

    for k in range(1, 8):
        to_z(k).start()

    net = Net(send_sems, recv_sems)
    state = {"at": False, "ready": [], "count": 0}
    colbuf_row = colbuf.at[dp]

    def product(left, right, c, out):
        out[...] = jnp.zeros_like(out)

        def step(k, carry):
            s = pl.multiple_of(k * 512, 512)
            out[...] += jnp.dot(left[:, pl.ds(s, 512)], right[c, pl.ds(s, 512), :],
                                preferred_element_type=F32)
            return carry

        lax.fori_loop(0, 8, step, 0)

    def gradient(c):
        net.now += DOT_US
        product(at, ob, c, g_v.at[c])
        squares = g_v[c] * g_v[c] + tiny_square
        colbuf_row[:, pl.ds(c * W, W)] = jnp.sum(squares, axis=0, keepdims=True)
        if state["count"] == 0:
            h_v[...] = squares
        else:
            h_v[...] += squares
        state["count"] += 1

    def chunk_here(c):
        if state["at"]:
            gradient(c)
        else:
            state["ready"].append(c)

    def at_here():
        state["at"] = True
        for c in state["ready"]:
            gradient(c)

    first = GatherDp(net, me, ob, o_relay, chunk_here)
    for c in Y_FIRST:
        loads[3 + c].wait()
        first.along_y(c, False)
        first.along_x(c, 0, 0)
        first.along_x(c, 0, 1)
    for k in range(1, 8):
        to_z(k).wait_recv()
    for k in range(1, 8):
        to_dp(k).start()
    at[pl.ds(strip_row, 16), pl.ds(pl.multiple_of(dp * ROWS, ROWS), ROWS)] = pieces[dp]
    net.now = 5.0
    for c in X_FIRST:
        loads[3 + c].wait()
        first.along_x(c, 0, 0)
        first.along_x(c, 0, 1)
        first.along_y(c, False)

    def strip_x(z, xl, core):
        return xb.at[:, pl.ds(pl.multiple_of((4 * z + 2 * xl + core) * W, W), W)]

    def strip_a(z, xl, core):
        return at.at[pl.ds(pl.multiple_of((2 * xl + core) * W + 16 * z, 16), 16), :]

    for k in range(1, 8):
        to_dp(k).wait_recv()
    GatherMp(net, me, strip_a, {1: 4, -1: 3}, at_here).start()
    loads[1].wait()
    GatherMp(net, me, strip_x, {1: 3, -1: 4}, lambda: None).start()

    loads[2].wait()
    wsq = jnp.zeros((8, 128), F32)

    def weight_step(k, carry):
        w = w_v[pl.ds(pl.multiple_of(k * 8, 8), 8), :]
        w = w * w
        for c in range(CHUNKS):
            carry = carry + w[:, c * W:(c + 1) * W]
        return carry

    wsq = lax.fori_loop(0, ROWS // 8, weight_step, wsq)
    wsum = jnp.sum(wsq, axis=0, keepdims=True)

    net.run()

    def to_all(buf, mine, axis, size, send, recv):
        def copy(k):
            device = ((mine + k) % size, mp) if axis == "dp" else (dp, (mine + k) % size)
            return pltpu.make_async_remote_copy(
                src_ref=buf.at[mine], dst_ref=buf.at[mine], send_sem=send.at[k], recv_sem=recv.at[k],
                device_id=device, device_id_type=MESH)

        def start(k, carry):
            copy(k).start()
            return carry

        def wait(k, carry):
            copy(k).wait_recv()
            return carry

        def wait_sent(k, carry):
            copy(k).wait_send()
            return carry

        return (lambda: lax.fori_loop(1, size, start, 0), lambda: lax.fori_loop(1, size, wait, 0),
                lambda: lax.fori_loop(1, size, wait_sent, 0))

    col_start, col_wait, col_sent = to_all(colbuf, dp, "dp", 8, col_send, col_recv)
    row_start, row_wait, row_sent = to_all(rowbuf, mp, "mp", 32, row_send, row_recv)
    t_start, t_wait, t_sent = to_all(tbuf, mp, "mp", 32, t_send, t_recv)
    last_start, last_wait, last_sent = to_all(lastbuf, dp, "dp", 8, last_send, last_recv)

    col_start()
    my_row = rowbuf.at[mp]
    my_row[:, :ROWS] = jnp.sum(h_v[...].T, axis=0, keepdims=True)
    my_row[:, ROWS:] = wsum
    row_start()
    col_wait()
    column_moment = decay_rate * col_state[...] + (1.0 - decay_rate) * (
        jnp.sum(colbuf[...], axis=0) / D)
    col_out[...] = column_moment
    inverse = 1.0 / column_moment
    for c in range(CHUNKS):
        term = g_v[c] * g_v[c] * inverse[:, c * W:(c + 1) * W]
        if c == 0:
            h_v[...] = term
        else:
            h_v[...] += term
    my_t = tbuf.at[mp]
    my_t[...] = jnp.sum(h_v[...].T, axis=0, keepdims=True)
    t_start()
    row_wait()
    rows = jnp.sum(rowbuf[...], axis=0)
    row_moment = decay_rate * row_state[...] + (1.0 - decay_rate) * (rows[:, :ROWS] / FF)
    row_out[...] = row_moment
    t_wait()
    terms = jnp.sum(tbuf[...], axis=0) / row_moment
    last = lastbuf.at[dp]
    last[:, :W] = terms[:, :128] + terms[:, 128:256] + terms[:, 256:384] + terms[:, 384:]
    last[:, W:] = rows[:, ROWS:]
    last_start()
    h_v[...] = jnp.broadcast_to(lax.rsqrt(row_moment), (W, ROWS)).T
    col_scale = lax.rsqrt(column_moment)
    last_wait()
    totals = jnp.sum(lastbuf[...], axis=0)
    raw_total = jnp.sum(totals[:, :W], axis=1, keepdims=True)
    weight_total = jnp.sum(totals[:, W:], axis=1, keepdims=True)
    rms_update = jnp.sqrt(raw_total / (D * FF))
    shrink = 1.0 / jnp.maximum(1.0, rms_update / clip_level)
    rms_weight = jnp.sqrt(weight_total / (D * FF) + weight_eps)
    rate = learn_rate * rms_weight

    second_net = Net(send_sems, recv_sems)
    net.finish()

    def hidden_here(c):
        second_net.now += DOT_US
        product(xb, wb, c, h_v)
        nxt_v[:, c * W:(c + 1) * W] = h_v[...].astype(BF16)
        stores.append(pltpu.make_async_copy(
            nxt_v.at[:, pl.ds(c * W, W)], hidden.at[:, pl.ds(c * W, W)], local_sems.at[c]))
        stores[-1].start()

    stores = []
    second = GatherDp(second_net, me, wb, w_relay, hidden_here)
    for c in Y_FIRST + X_FIRST:
        cols = slice(c * W, (c + 1) * W)
        upd = g_v[c] * h_v[...] * (col_scale[:, cols] * shrink)
        u_v[:, cols] = upd
        fresh = w_v[:, cols] - rate * upd
        w_v[:, cols] = fresh
        block(wb, c, dp)[...] = fresh.astype(BF16)
        if c in Y_FIRST:
            second.along_y(c, False)
        second.along_x(c, 0, 0)
        second.along_x(c, 0, 1)
        if c in X_FIRST:
            second.along_y(c, False)
    stores.append(pltpu.make_async_copy(u_v, update, local_sems.at[8]))
    stores.append(pltpu.make_async_copy(w_v, new_weight, local_sems.at[9]))
    stores[0].start()
    stores[1].start()
    second_net.run()
    second_net.finish()
    for k in range(1, 8):
        to_z(k).wait_send()
        to_dp(k).wait_send()
    col_sent()
    row_sent()
    t_sent()
    last_sent()
    for copy in stores:
        copy.wait()


def body(activations, out_grads, weight, row_state, column_state, next_batch):
    any_space = pl.BlockSpec(memory_space=pl.ANY)
    vmem = pl.BlockSpec(memory_space=pltpu.VMEM)
    dma = pltpu.SemaphoreType.DMA
    new_weight, update, row_moment, column_moment, hidden = pl.pallas_call(
        kernel,
        name="adafactor",
        out_shape=(
            jax.ShapeDtypeStruct((ROWS, COLS), F32),
            jax.ShapeDtypeStruct((ROWS, COLS), F32),
            jax.ShapeDtypeStruct((1, ROWS), F32),
            jax.ShapeDtypeStruct((1, COLS), F32),
            jax.ShapeDtypeStruct((ROWS, COLS), BF16),
        ),
        in_specs=[any_space, any_space, any_space, vmem, vmem, any_space],
        out_specs=(any_space, any_space, vmem, vmem, any_space),
        scratch_shapes=[
            pltpu.VMEM((ROWS, W), BF16),
            pltpu.VMEM((ROWS, COLS), BF16),
            pltpu.VMEM((W, ROWS), BF16),
            pltpu.VMEM((8, 16, ROWS), BF16),
            pltpu.VMEM((ROWS, D), BF16),
            pltpu.VMEM((ROWS, D), BF16),
            pltpu.VMEM((CHUNKS, D, W), BF16),
            pltpu.VMEM((CHUNKS, D, W), BF16),
            pltpu.VMEM((RELAYS, ROWS // 2, W), BF16),
            pltpu.VMEM((RELAYS, ROWS // 2, W), BF16),
            pltpu.VMEM((ROWS, COLS), F32),
            pltpu.VMEM((CHUNKS, ROWS, W), F32),
            pltpu.VMEM((ROWS, COLS), F32),
            pltpu.VMEM((ROWS, W), F32),
            pltpu.VMEM((8, 1, COLS), F32),
            pltpu.VMEM((32, 1, ROWS + W), F32),
            pltpu.VMEM((32, 1, ROWS), F32),
            pltpu.VMEM((8, 1, 2 * W), F32),
            dma((COPIES,)), dma((COPIES,)),
            dma((8,)), dma((8,)), dma((8,)), dma((8,)),
            dma((8,)), dma((8,)), dma((32,)), dma((32,)),
            dma((32,)), dma((32,)), dma((8,)), dma((8,)),
            dma((11,)),
        ],
        compiler_params=pltpu.CompilerParams(
            collective_id=0, has_side_effects=True, vmem_limit_bytes=60 * 1024 * 1024),
    )(activations, out_grads, weight, row_state.reshape(1, ROWS), column_state.reshape(1, COLS), next_batch)
    return new_weight, update, row_moment.reshape(ROWS), column_moment.reshape(COLS), hidden


def solution(mesh):
    return jax.shard_map(
        body,
        mesh=mesh,
        in_specs=(P("dp", "mp"), P("dp", "mp"), P("dp", "mp"), P("dp"), P("mp"), P("dp", "mp")),
        out_specs=(P("dp", "mp"), P("dp", "mp"), P("dp"), P("mp"), P("dp", "mp")),
        check_vma=False,
    )
```

```python
import functools
import heapq

import jax
import jax.numpy as jnp
from jax import lax
from jax.experimental import pallas as pl
from jax.experimental.pallas import tpu as pltpu
from jax.sharding import PartitionSpec as P

D = 4096
FF = 32768

tiny_square = 1e-30
weight_eps = 1e-06
decay_rate = 0.5
clip_level = 0.5
learn_rate = 0.01

ROWS = 512
COLS = 1024
W = 128
CHUNKS = COLS // W
Y_FIRST = (0, 1, 2)
X_FIRST = (3, 4, 5, 6, 7)
COPIES = 400
RELAYS = 2 * (len(X_FIRST) + 4 * len(Y_FIRST))

HOP_US = 1.7
RATE = 46e3
DOT_US = 0.2

F32 = jnp.float32
BF16 = jnp.bfloat16
MESH = pl.DeviceIdType.MESH


class Place:
    def __init__(self):
        self.dp = lax.axis_index("dp")
        self.mp = lax.axis_index("mp")
        self.y = self.dp // 2
        self.xh = self.dp % 2
        self.z = self.mp // 4
        self.xl = (self.mp // 2) % 2
        self.core = self.mp % 2
        self.x = 2 * self.xh + self.xl

    def device(self, dy=0, dx=0, dz=0, dcore=0):
        y = (self.y + dy) % 4
        x = (self.x + dx) % 4
        z = (self.z + dz) % 8
        core = (self.core + dcore) % 2
        return (2 * y + x // 2, 4 * z + 2 * (x % 2) + core)


class Net:
    def __init__(self, send_sems, recv_sems):
        self.send_sems, self.recv_sems = send_sems, recv_sems
        self.copies, self.heap, self.free = [], [], {}
        self.now = 0.0
        self.first = 0
        self.idle = None

    def send(self, link, src, dst, device, size, then, hop=HOP_US):
        k = len(self.copies)
        copy = pltpu.make_async_remote_copy(
            src_ref=src, dst_ref=dst, send_sem=self.send_sems.at[k], recv_sem=self.recv_sems.at[k],
            device_id=device, device_id_type=MESH)
        copy.start()
        self.copies.append(copy)
        begin = max(self.free.get(link, 0.0), self.now)
        end = begin + size / (RATE * (12 if link == "core" else 1))
        self.free[link] = end
        heapq.heappush(self.heap, (end + hop, k, copy, then))

    def run(self, until=None):
        while self.heap and not (until and until()):
            at, _, copy, then = heapq.heappop(self.heap)
            self.now = max(self.now, at)
            copy.wait_recv()
            if then is not None:
                then()
            if self.idle is not None:
                self.idle(2)
        if self.idle is not None:
            self.idle(1000)

    def finish(self):
        for copy in self.copies[self.first:]:
            copy.wait_send()
        self.first = len(self.copies)


def block(ref, c, t, half=None):
    if half is None:
        return ref.at[c, pl.ds(pl.multiple_of(t * ROWS, ROWS), ROWS), :]
    rows = ROWS // 2
    return ref.at[c, pl.ds(pl.multiple_of(t * ROWS + half * rows, rows), rows), :]


class Products:
    def __init__(self, net, step, done):
        self.net, self.step, self.done = net, step, done
        self.queue, self.ready = [], False
        self.left = {c: 16 for c in range(CHUNKS)}
        net.idle = self.advance

    def add(self, c, t, half=None):
        self.queue.append((c, t, half))

    def advance(self, count):
        while self.ready and self.queue and count:
            count -= 1
            c, t, half = self.queue.pop(0)
            self.step(c, t, half, self.left[c] == 16)
            self.net.now += DOT_US if half is None else DOT_US / 2
            self.left[c] -= 2 if half is None else 1
            if self.left[c] == 0:
                self.done(c)


class GatherDp:
    FULL = ROWS * W * 2

    def __init__(self, net, me, buf, relay, got):
        self.net, self.me, self.buf, self.relay, self.got = net, me, buf, relay, got
        self.relays = 0
        self.partner_halves = {c: 0 for c in X_FIRST}

    def index(self, dy, other):
        xh = (self.me.xh + 1) % 2 if other else self.me.xh
        return 2 * ((self.me.y + dy) % 4) + xh

    def along_y(self, c, other):
        for sign in (1, -1):
            part = block(self.buf, c, self.index(0, other))
            self.net.send(("y", sign), part, part, self.me.device(dy=sign), self.FULL,
                          functools.partial(self.from_y, c, other, sign))

    def from_y(self, c, other, sign):
        half = 0 if sign == 1 else 1
        part = block(self.buf, c, self.index(-sign, other), half)
        self.net.send(("y", sign), part, part, self.me.device(dy=sign), self.FULL // 2,
                      functools.partial(self.from_far_y, c, other, half))
        if c in Y_FIRST:
            self.along_x(c, -sign, 0)
            self.along_x(c, -sign, 1)
        self.got(c, self.index(-sign, other))

    def from_far_y(self, c, other, half):
        if c in Y_FIRST:
            self.along_x(c, 2, half)
        self.got(c, self.index(2, other), half)

    def along_x(self, c, dy, half):
        sign = 1 if half == 0 else -1
        slot = self.relay.at[self.relays]
        self.relays += 1
        self.net.send(("x", sign), block(self.buf, c, self.index(dy, False), half), slot,
                      self.me.device(dx=sign), self.FULL // 2,
                      functools.partial(self.relayed, c, dy, half, sign, slot))

    def relayed(self, c, dy, half, sign, slot):
        xh = ((self.me.x + 4 - sign) % 4) // 2
        t = 2 * ((self.me.y + dy) % 4) + xh
        self.net.send(("x", sign), slot, block(self.buf, c, t, half), self.me.device(dx=sign),
                      self.FULL // 2, functools.partial(self.from_x, c, dy, half))

    def from_x(self, c, dy, half):
        if c in X_FIRST:
            self.partner_halves[c] += 1
            if self.partner_halves[c] == 2:
                self.along_y(c, True)
        self.got(c, self.index(dy, True), half)


class GatherMp:
    SIZE = ROWS * W * 2

    def __init__(self, net, me, strip, reach, done):
        self.net, self.me, self.strip, self.reach, self.done = net, me, strip, reach, done
        self.left = 31

    def got(self):
        self.left -= 1
        if self.left == 0:
            self.done()

    def place(self, dz, other):
        xl = (self.me.xl + 1) % 2 if other else self.me.xl
        return self.strip((self.me.z + dz) % 8, xl, self.me.core)

    def start(self):
        mine = self.place(0, False)
        dp, z, xl, core = self.me.dp, self.me.z, (self.me.xl + 1) % 2, self.me.core
        self.net.send(("x", 0), mine, mine, (dp, 4 * z + 2 * xl + core), self.SIZE, self.pair)
        self.have(0, False)

    def pair(self):
        self.have(0, True)
        self.got()

    def have(self, dz, other):
        part = self.place(dz, other)
        for sign in (1, -1):
            hops = -dz * sign
            if (dz == 0 or hops > 0) and hops < self.reach[sign]:
                self.net.send(("z", sign), part, part, self.me.device(dz=sign), self.SIZE,
                              functools.partial(self.from_z, dz - sign, other))
        self.net.send("core", part, part, self.me.device(dcore=1), self.SIZE, self.got, hop=1.0)

    def from_z(self, dz, other):
        self.have(dz, other)
        self.got()


def kernel(act, out_grads, weight, row_state, col_state, nxt,
           new_weight, update, row_out, col_out, hidden,
           act_v, nxt_v, act_t, pieces, at, xb, ob, wb, o_relay, w_relay,
           w_v, g_v, u_v, h_v, colbuf, rowbuf, tbuf, lastbuf,
           send_sems, recv_sems, a_send, a_recv, b_send, b_recv,
           col_send, col_recv, row_send, row_recv, t_send, t_recv, last_send, last_recv, local_sems):
    me = Place()
    dp, mp = me.dp, me.mp

    loads = [
        pltpu.make_async_copy(act, act_v, local_sems.at[0]),
        pltpu.make_async_copy(nxt, xb.at[:, pl.ds(pl.multiple_of(mp * W, W), W)], local_sems.at[1]),
        pltpu.make_async_copy(weight, w_v, local_sems.at[2]),
    ]
    for c in range(CHUNKS):
        loads.append(pltpu.make_async_copy(
            out_grads.at[:, pl.ds(c * W, W)], block(ob, c, dp), local_sems.at[3 + c]))
    for copy in loads:
        copy.start()

    barrier = pltpu.get_barrier_semaphore()

    def greet_mp(k, carry):
        pl.semaphore_signal(barrier, inc=1, device_id=(dp, (mp + k) % 32), device_id_type=MESH)
        return carry

    def greet_dp(k, carry):
        pl.semaphore_signal(barrier, inc=1, device_id=((dp + k) % 8, mp), device_id_type=MESH)
        return carry

    lax.fori_loop(1, 32, greet_mp, 0)
    lax.fori_loop(1, 8, greet_dp, 0)
    pl.semaphore_signal(barrier, inc=1, device_id=me.device(dx=2 * me.xl - 1), device_id_type=MESH)

    loads[0].wait()
    act_t[...] = act_v[...].T
    pieces[me.z] = act_t[pl.ds(pl.multiple_of(16 * me.z, 16), 16), :]
    pl.semaphore_wait(barrier, 39)

    def to_z(k):
        z = (me.z + k) % 8
        return pltpu.make_async_remote_copy(
            src_ref=act_t.at[pl.ds(pl.multiple_of(16 * z, 16), 16), :], dst_ref=pieces.at[me.z],
            send_sem=a_send.at[k], recv_sem=a_recv.at[k],
            device_id=(dp, (mp + 4 * k) % 32), device_id_type=MESH)

    strip_row = pl.multiple_of((2 * me.xl + me.core) * W + 16 * me.z, 16)

    def to_dp(k):
        i = (dp + k) % 8
        return pltpu.make_async_remote_copy(
            src_ref=pieces.at[i],
            dst_ref=at.at[pl.ds(strip_row, 16), pl.ds(pl.multiple_of(dp * ROWS, ROWS), ROWS)],
            send_sem=b_send.at[k], recv_sem=b_recv.at[k],
            device_id=(i, mp), device_id_type=MESH)

    for k in range(1, 8):
        to_z(k).start()

    net = Net(send_sems, recv_sems)
    state = {"count": 0}
    colbuf_row = colbuf.at[dp]

    def product(left, right):
        def step(c, t, half, first):
            size = ROWS if half is None else ROWS // 2
            s = pl.multiple_of(t * ROWS + (half or 0) * size, size)

            def rows(k, carry):
                r = pl.multiple_of(k * 256, 256)
                part = jnp.dot(left[pl.ds(r, 256), pl.ds(s, size)], right[c, pl.ds(s, size), :],
                               preferred_element_type=F32)
                if first:
                    g_v[c, pl.ds(r, 256), :] = part
                else:
                    g_v[c, pl.ds(r, 256), :] += part
                return carry

            lax.fori_loop(0, ROWS // 256, rows, 0)

        return step

    def gradient(c):
        squares = g_v[c] * g_v[c] + tiny_square
        colbuf_row[:, pl.ds(c * W, W)] = jnp.sum(squares, axis=0, keepdims=True)
        if state["count"] == 0:
            h_v[...] = squares
        else:
            h_v[...] += squares
        state["count"] += 1

    products = Products(net, product(at, ob), gradient)

    def at_here():
        products.ready = True

    loads[2].wait()
    wsq = jnp.zeros((8, 128), F32)

    def weight_step(k, carry):
        w = w_v[pl.ds(pl.multiple_of(k * 8, 8), 8), :]
        w = w * w
        for c in range(CHUNKS):
            carry = carry + w[:, c * W:(c + 1) * W]
        return carry

    wsq = lax.fori_loop(0, ROWS // 8, weight_step, wsq)
    wsum = jnp.sum(wsq, axis=0, keepdims=True)

    first = GatherDp(net, me, ob, o_relay, products.add)
    for k in range(1, 8):
        to_z(k).wait_recv()
    for k in range(1, 8):
        to_dp(k).start()
    at[pl.ds(strip_row, 16), pl.ds(pl.multiple_of(dp * ROWS, ROWS), ROWS)] = pieces[dp]
    for c in Y_FIRST + X_FIRST:
        loads[3 + c].wait()
        products.add(c, dp)
        if c in Y_FIRST:
            first.along_y(c, False)
        first.along_x(c, 0, 0)
        first.along_x(c, 0, 1)
        if c in X_FIRST:
            first.along_y(c, False)
    net.now = 5.0

    def strip_x(z, xl, core):
        return xb.at[:, pl.ds(pl.multiple_of((4 * z + 2 * xl + core) * W, W), W)]

    def strip_a(z, xl, core):
        return at.at[pl.ds(pl.multiple_of((2 * xl + core) * W + 16 * z, 16), 16), :]

    for k in range(1, 8):
        to_dp(k).wait_recv()
    GatherMp(net, me, strip_a, {1: 4, -1: 3}, at_here).start()
    loads[1].wait()
    GatherMp(net, me, strip_x, {1: 3, -1: 4}, lambda: None).start()

    net.run()

    def to_all(buf, mine, axis, size, send, recv):
        def copy(k):
            device = ((mine + k) % size, mp) if axis == "dp" else (dp, (mine + k) % size)
            return pltpu.make_async_remote_copy(
                src_ref=buf.at[mine], dst_ref=buf.at[mine], send_sem=send.at[k], recv_sem=recv.at[k],
                device_id=device, device_id_type=MESH)

        def start(k, carry):
            copy(k).start()
            return carry

        def wait(k, carry):
            copy(k).wait_recv()
            return carry

        def wait_sent(k, carry):
            copy(k).wait_send()
            return carry

        return (lambda: lax.fori_loop(1, size, start, 0), lambda: lax.fori_loop(1, size, wait, 0),
                lambda: lax.fori_loop(1, size, wait_sent, 0))

    col_start, col_wait, col_sent = to_all(colbuf, dp, "dp", 8, col_send, col_recv)
    row_start, row_wait, row_sent = to_all(rowbuf, mp, "mp", 32, row_send, row_recv)
    t_start, t_wait, t_sent = to_all(tbuf, mp, "mp", 32, t_send, t_recv)
    last_start, last_wait, last_sent = to_all(lastbuf, dp, "dp", 8, last_send, last_recv)

    col_start()
    my_row = rowbuf.at[mp]
    my_row[:, :ROWS] = jnp.sum(h_v[...].T, axis=0, keepdims=True)
    my_row[:, ROWS:] = wsum
    row_start()
    col_wait()
    column_moment = decay_rate * col_state[...] + (1.0 - decay_rate) * (
        jnp.sum(colbuf[...], axis=0) / D)
    col_out[...] = column_moment
    inverse = 1.0 / column_moment
    for c in range(CHUNKS):
        term = g_v[c] * g_v[c] * inverse[:, c * W:(c + 1) * W]
        if c == 0:
            h_v[...] = term
        else:
            h_v[...] += term
    my_t = tbuf.at[mp]
    my_t[...] = jnp.sum(h_v[...].T, axis=0, keepdims=True)
    t_start()
    row_wait()
    rows = jnp.sum(rowbuf[...], axis=0)
    row_moment = decay_rate * row_state[...] + (1.0 - decay_rate) * (rows[:, :ROWS] / FF)
    row_out[...] = row_moment
    t_wait()
    terms = jnp.sum(tbuf[...], axis=0) / row_moment
    last = lastbuf.at[dp]
    last[:, :W] = terms[:, :128] + terms[:, 128:256] + terms[:, 256:384] + terms[:, 384:]
    last[:, W:] = rows[:, ROWS:]
    last_start()
    h_v[...] = jnp.broadcast_to(lax.rsqrt(row_moment), (W, ROWS)).T
    col_scale = lax.rsqrt(column_moment)
    last_wait()
    totals = jnp.sum(lastbuf[...], axis=0)
    raw_total = jnp.sum(totals[:, :W], axis=1, keepdims=True)
    weight_total = jnp.sum(totals[:, W:], axis=1, keepdims=True)
    rms_update = jnp.sqrt(raw_total / (D * FF))
    shrink = 1.0 / jnp.maximum(1.0, rms_update / clip_level)
    rms_weight = jnp.sqrt(weight_total / (D * FF) + weight_eps)
    rate = learn_rate * rms_weight

    second_net = Net(send_sems, recv_sems)
    net.finish()

    def hidden_here(c):
        nxt_v[:, c * W:(c + 1) * W] = g_v[c].astype(BF16)
        stores.append(pltpu.make_async_copy(
            nxt_v.at[:, pl.ds(c * W, W)], hidden.at[:, pl.ds(c * W, W)], local_sems.at[c]))
        stores[-1].start()

    stores = []
    products = Products(second_net, product(xb, wb), hidden_here)
    second = GatherDp(second_net, me, wb, w_relay, products.add)
    for c in Y_FIRST + X_FIRST:
        cols = slice(c * W, (c + 1) * W)
        upd = g_v[c] * h_v[...] * (col_scale[:, cols] * shrink)
        u_v[:, cols] = upd
        fresh = w_v[:, cols] - rate * upd
        w_v[:, cols] = fresh
        block(wb, c, dp)[...] = fresh.astype(BF16)
        products.add(c, dp)
        if c in Y_FIRST:
            second.along_y(c, False)
        second.along_x(c, 0, 0)
        second.along_x(c, 0, 1)
        if c in X_FIRST:
            second.along_y(c, False)
    stores.append(pltpu.make_async_copy(u_v, update, local_sems.at[8]))
    stores.append(pltpu.make_async_copy(w_v, new_weight, local_sems.at[9]))
    stores[0].start()
    stores[1].start()
    products.ready = True
    second_net.run()
    second_net.finish()
    for k in range(1, 8):
        to_z(k).wait_send()
        to_dp(k).wait_send()
    col_sent()
    row_sent()
    t_sent()
    last_sent()
    for copy in stores:
        copy.wait()


def body(activations, out_grads, weight, row_state, column_state, next_batch):
    any_space = pl.BlockSpec(memory_space=pl.ANY)
    vmem = pl.BlockSpec(memory_space=pltpu.VMEM)
    dma = pltpu.SemaphoreType.DMA
    new_weight, update, row_moment, column_moment, hidden = pl.pallas_call(
        kernel,
        name="adafactor",
        out_shape=(
            jax.ShapeDtypeStruct((ROWS, COLS), F32),
            jax.ShapeDtypeStruct((ROWS, COLS), F32),
            jax.ShapeDtypeStruct((1, ROWS), F32),
            jax.ShapeDtypeStruct((1, COLS), F32),
            jax.ShapeDtypeStruct((ROWS, COLS), BF16),
        ),
        in_specs=[any_space, any_space, any_space, vmem, vmem, any_space],
        out_specs=(any_space, any_space, vmem, vmem, any_space),
        scratch_shapes=[
            pltpu.VMEM((ROWS, W), BF16),
            pltpu.VMEM((ROWS, COLS), BF16),
            pltpu.VMEM((W, ROWS), BF16),
            pltpu.VMEM((8, 16, ROWS), BF16),
            pltpu.VMEM((ROWS, D), BF16),
            pltpu.VMEM((ROWS, D), BF16),
            pltpu.VMEM((CHUNKS, D, W), BF16),
            pltpu.VMEM((CHUNKS, D, W), BF16),
            pltpu.VMEM((RELAYS, ROWS // 2, W), BF16),
            pltpu.VMEM((RELAYS, ROWS // 2, W), BF16),
            pltpu.VMEM((ROWS, COLS), F32),
            pltpu.VMEM((CHUNKS, ROWS, W), F32),
            pltpu.VMEM((ROWS, COLS), F32),
            pltpu.VMEM((ROWS, W), F32),
            pltpu.VMEM((8, 1, COLS), F32),
            pltpu.VMEM((32, 1, ROWS + W), F32),
            pltpu.VMEM((32, 1, ROWS), F32),
            pltpu.VMEM((8, 1, 2 * W), F32),
            dma((COPIES,)), dma((COPIES,)),
            dma((8,)), dma((8,)), dma((8,)), dma((8,)),
            dma((8,)), dma((8,)), dma((32,)), dma((32,)),
            dma((32,)), dma((32,)), dma((8,)), dma((8,)),
            dma((11,)),
        ],
        compiler_params=pltpu.CompilerParams(
            collective_id=0, has_side_effects=True, vmem_limit_bytes=60 * 1024 * 1024),
    )(activations, out_grads, weight, row_state.reshape(1, ROWS), column_state.reshape(1, COLS), next_batch)
    return new_weight, update, row_moment.reshape(ROWS), column_moment.reshape(COLS), hidden


def solution(mesh):
    return jax.shard_map(
        body,
        mesh=mesh,
        in_specs=(P("dp", "mp"), P("dp", "mp"), P("dp", "mp"), P("dp"), P("mp"), P("dp", "mp")),
        out_specs=(P("dp", "mp"), P("dp", "mp"), P("dp"), P("mp"), P("dp", "mp")),
        check_vma=False,
    )
```
